32 devices in a mesh: group: 4 (over x, core), replica: 8 (over z, y).
Axes of the slice: x: 2, y: 2, z: 4, core: 2. Of those that a mesh axis runs over, the one named last changes fastest.
Arguments:
- grad_parts: bfloat16 [8, 8, 128, 512], P('replica', None, 'group'), may hold values from -1 to 1
- owner_order: int32 [8], replicated, may hold values from 0 to 7, each once
- step_count: int32 [1], replicated, may hold values from 1 to 12
- stat_old: float32 [8, 512, 512], P('replica'), as said below
- root_old: bfloat16 [8, 512, 512], P('replica'), may hold values from -0.25 to 0.25
Outputs:
- update: bfloat16 [8, 128, 512], P(None, 'group')
- stat_new: float32 [8, 512, 512], P('replica')
- root_new: bfloat16 [8, 512, 512], P('replica')
The draws below stay inside these ranges and needn't reach their ends.
Inputs may be any that keep to these rules, and one draw needn't show every extreme that they name: `stat_old`: each matrix is symmetric positive definite.
All inputs are finite; a program needn't handle non-finite values.
Results may differ from the reference program's by a relative error of at most 0.001.
The reference program's roundings to bfloat16 on the way count: a program that leaves them out, or rounds other values in their place, can miss the bound.
Values may be sent and summed in bfloat16 or wider, within the bound.
No kernel may reach another device: no remote copies, remote signals or barrier semaphores. Data moves between devices by JAX's collectives and lax.ppermute only.
A program may use at most 64 MiB of HBM per device.

```python
import jax
import jax.numpy as jnp
from jax import lax

BW = 512
ITERS = 3
NBLK = 8
ROWS = 128
N_REPLICA = 8


def draw_stat_old(key, part):
    first = jax.random.fold_in(jax.random.fold_in(key, 7), 0)
    factor = jax.random.normal(first, (NBLK, BW, BW), jnp.float32)
    product = jnp.einsum('bik,bjk->bij', factor, factor)
    return product * (ROWS / BW) + 0.1 * ROWS * jnp.eye(BW, dtype=jnp.float32)


def spiked(entries, rng, source, target, blocks, factor):
    def block_of(axis_at):
        return (jnp.arange(entries.shape[axis_at]) // (entries.shape[axis_at] // blocks)).reshape((-1,) + (1,) * (entries.ndim - 1 - axis_at))

    near = jax.random.permutation(rng, blocks)[block_of(target)]
    other_side = (block_of(target) + blocks // 2) % blocks
    return jnp.where((block_of(source) == near) | (block_of(source) == other_side), factor * entries, entries)


def level_of(rng, dims, pieces, low, high):
    gain, own = 1.0, jax.random.fold_in(rng, 6)
    for dim, shards_of in pieces:
        draws = jnp.exp(jax.random.uniform(jax.random.fold_in(own, dim), (shards_of,), jnp.float32, low / len(pieces), high / len(pieces)))
        gain = gain * jnp.repeat(draws, dims[dim] // shards_of).reshape([-1 if axis == dim else 1 for axis in range(len(dims))])
    return gain


def scatter_about(key, shape, spread, most, cuts=(), kind=jnp.bfloat16):
    array = spread * jax.random.normal(key, shape, jnp.float32)
    if cuts:
        array = array * level_of(key, shape, cuts, -0.22, 0.18)
    return jnp.clip(array, -most, most).astype(kind)


def heavy_noise(stream_key, dims, scale, most, shards, heavy, kind=jnp.bfloat16):
    entries = scale * jax.random.normal(stream_key, dims, jnp.float32)
    if shards:
        entries = entries * level_of(stream_key, dims, shards, -0.22, 0.18)
    return jnp.clip(spiked(entries, jax.random.fold_in(stream_key, 3), *heavy), -most, most).astype(kind)


def setup_inputs(seed: int = 0) -> dict:
    keys = jax.random.split(jax.random.key(seed), 6)
    grad_parts = heavy_noise(keys[0], (N_REPLICA, NBLK, ROWS, BW), 0.15, 1.0, ((0, 8), (2, 4)), (0, 1, 8, 2.0))
    owner_order = jax.random.permutation(keys[1], NBLK).astype(jnp.int32)
    step_count = jax.random.randint(keys[2], (1,), 1, 13).astype(jnp.int32)
    stat_old = draw_stat_old(jax.random.fold_in(keys[5], 71), 0)
    root_old = scatter_about(keys[4], (NBLK, BW, BW), BW ** -0.5, 0.25, ((0, 8),))
    return dict(grad_parts=grad_parts, owner_order=owner_order, step_count=step_count, stat_old=stat_old, root_old=root_old)


decay_rate = 0.95
epsilon = 0.001

def newton(shifted):
    identity = jnp.eye(BW, dtype=jnp.float32)
    frobenius = jnp.sqrt(jnp.sum(shifted * shifted))
    coupled = shifted / frobenius
    root_iter = identity * frobenius ** (-0.25)
    for repeat in range(ITERS):
        factor = (5.0 * identity - coupled) * 0.25
        root_iter = jnp.dot(root_iter, factor, precision=lax.Precision.HIGHEST)
        if repeat + 1 < ITERS:
            factor_sq = jnp.dot(factor, factor, precision=lax.Precision.HIGHEST)
            factor_quad = jnp.dot(factor_sq, factor_sq, precision=lax.Precision.HIGHEST)
            coupled = jnp.dot(factor_quad, coupled, precision=lax.Precision.HIGHEST)
    return root_iter

def reference(grad_parts, owner_order, step_count, stat_old, root_old):

    def add_one(replica_index, running):
        return running + grad_parts[replica_index].astype(jnp.float32)
    summed = lax.fori_loop(0, N_REPLICA, add_one, jnp.zeros((NBLK, ROWS, BW), jnp.float32))
    slot_grads = summed[owner_order]
    gram_matrix = jnp.einsum('bri,brj->bij', slot_grads, slot_grads, precision=lax.Precision.HIGHEST)
    rounded = slot_grads.astype(jnp.bfloat16).astype(jnp.float32)
    products = jnp.einsum('bri,bij->brj', rounded, root_old.astype(jnp.float32))
    grad_norm = jnp.trace(gram_matrix, axis1=1, axis2=2)
    update_norm = lax.optimization_barrier(jnp.sum(products * products, axis=(1, 2)))
    graft_scale = jnp.sqrt(grad_norm / (update_norm + 1e-06))
    scaled = (graft_scale[:, None, None] * products).astype(jnp.bfloat16)
    update = jnp.zeros_like(scaled).at[owner_order].set(scaled)
    stat_new = decay_rate * stat_old + (1.0 - decay_rate) * gram_matrix
    correction = 1.0 / (1.0 - decay_rate ** step_count[0].astype(jnp.float32))
    shifted = stat_new * correction + epsilon * jnp.eye(BW, dtype=jnp.float32)
    root_new = lax.map(newton, shifted).astype(jnp.bfloat16)
    return (update, stat_new, root_new)
```

```python
import functools

import jax
import jax.numpy as jnp
from jax import lax
from jax.experimental import pallas as pl
from jax.experimental.pallas import tpu as pltpu
from jax.sharding import PartitionSpec as P


decay_rate = 0.95
epsilon = 0.001

VMEM = pl.BlockSpec(memory_space=pltpu.VMEM)
SMEM = pl.BlockSpec(memory_space=pltpu.SMEM)
ANY = pl.BlockSpec(memory_space=pl.ANY)


def halves(size):
    inner = 2 if size % 2 == 0 else 1
    return size // inner, inner


def is_power(n):
    return n & (n - 1) == 0


def ahead(i, k, n):
    if is_power(n):
        return i ^ k
    return (i + k) % n


def behind(i, k, n):
    if is_power(n):
        return i ^ k
    return (i + n - k) % n


def traced_behind(i, k, n):
    return lax.bitwise_xor(i, jnp.int32(k)) if is_power(n) else lax.rem(i + (n - k), n)


def traced_ahead(i, k, n):
    return lax.bitwise_xor(i, jnp.int32(k)) if is_power(n) else lax.rem(i + k, n)


def send(x, groups, replicas, dg, dr):
    go, gi = halves(groups)
    ro, ri = halves(replicas)
    pairs = []
    for a in range(go):
        for b in range(gi):
            for c in range(ro):
                for d in range(ri):
                    source = (a * gi + b) * replicas + c * ri + d
                    other_group = ahead(a, dg[0], go) * gi + ahead(b, dg[1], gi)
                    other_replica = ahead(c, dr[0], ro) * ri + ahead(d, dr[1], ri)
                    pairs.append((source, other_group * replicas + other_replica))
    return lax.ppermute(x, ("group", "replica"), pairs)


def pick_kernel(replicas, order_ref, grads_ref, *rest):
    ro, ri = halves(replicas)
    outs, sem = rest[:-1], rest[-1]
    me = lax.axis_index("replica")
    outer, inner = lax.div(me, ri), lax.rem(me, ri)
    copies = []
    for k in range(ro):
        for d in range(ri):
            slot = traced_ahead(outer, k, ro) * ri + traced_ahead(inner, d, ri)
            copy = pltpu.make_async_copy(grads_ref.at[order_ref[slot]], outs[k].at[d], sem.at[k, d])
            copy.start()
            copies.append(copy)
    for copy in copies:
        copy.wait()


def place_kernel(replicas, order_ref, *rest):
    ro, ri = halves(replicas)
    blocks, out_ref, sem = rest[:ro], rest[ro], rest[ro + 1]
    me = lax.axis_index("replica")
    outer, inner = lax.div(me, ri), lax.rem(me, ri)
    copies = []
    for k in range(ro):
        for d in range(ri):
            slot = traced_behind(outer, k, ro) * ri + traced_behind(inner, d, ri)
            copy = pltpu.make_async_copy(blocks[k].at[d], out_ref.at[order_ref[slot]], sem.at[k, d])
            copy.start()
            copies.append(copy)
    for copy in copies:
        copy.wait()


def graft_kernel(rows, mine_ref, other_ref, root_ref, out_ref):
    mine = mine_ref[...]
    other = other_ref[...]
    root = root_ref[...]
    mine_products = jnp.dot(mine.astype(jnp.bfloat16), root, preferred_element_type=jnp.float32)
    other_products = jnp.dot(other.astype(jnp.bfloat16), root, preferred_element_type=jnp.float32)

    def total(a, b):
        lines = jnp.sum(a * a, axis=0, keepdims=True) + jnp.sum(b * b, axis=0, keepdims=True)
        return jnp.sum(lines, axis=1, keepdims=True)

    graft = jnp.sqrt(total(mine, other) / (total(mine_products, other_products) + 1e-06))
    out_ref[...] = (graft * mine_products[:rows]).astype(jnp.bfloat16)


def dot(a, b):
    return jnp.dot(a, b, preferred_element_type=jnp.float32)


def tiles(n):
    step = 128 if n % 128 == 0 else n
    return [slice(r, r + step) for r in range(0, n, step)]


def quintic(m_ref, mb_ref, w_ref, wb_ref, vb_ref, out_ref, outb_ref):
    n = m_ref.shape[0]
    for r in tiles(n):
        w = 10.0 * m_ref[r] - dot(mb_ref[r], mb_ref[...])
        w_ref[r] = w
        wb_ref[r] = w.astype(jnp.bfloat16)
    for r in tiles(n):
        vb_ref[r] = (dot(wb_ref[r], wb_ref[...]) - 50.0 * w_ref[r]).astype(jnp.bfloat16)
    for r in tiles(n):
        m = (625.0 * m_ref[r] + dot(vb_ref[r], mb_ref[...])) * (1.0 / 256.0)
        out_ref[r] = m
        outb_ref[r] = m.astype(jnp.bfloat16)


def eye_rows(r, n):
    rows = lax.broadcasted_iota(jnp.int32, (r.stop - r.start, n), 0) + r.start
    columns = lax.broadcasted_iota(jnp.int32, (r.stop - r.start, n), 1)
    return rows == columns


def stat_kernel(corr_ref, mine_ref, other_ref, stat_ref, stat_out, m0_ref, m1_ref, c_ref, m0b, w, wb, vb, m1b):
    n = stat_ref.shape[0]
    s = jnp.concatenate([mine_ref[...], other_ref[...]], axis=0)
    high = s.astype(jnp.bfloat16)
    low = (s - high.astype(jnp.float32)).astype(jnp.bfloat16)
    left = jnp.concatenate([high, low, high], axis=0)
    right = jnp.concatenate([high, high, low], axis=0)
    corr = corr_ref[0]
    total = jnp.zeros((1, n), jnp.float32)
    for r in tiles(n):
        gram = lax.dot_general(
            left[:, r], right, (((0,), (0,)), ((), ())), preferred_element_type=jnp.float32
        )
        stat = decay_rate * stat_ref[r] + (1.0 - decay_rate) * gram
        stat_out[r] = stat
        shifted = stat * corr + jnp.where(eye_rows(r, n), epsilon, 0.0)
        m0_ref[r] = shifted
        total += jnp.sum(shifted * shifted, axis=0, keepdims=True)
    frobenius = jnp.sqrt(jnp.sum(total, axis=1, keepdims=True))
    inverse = 1.0 / frobenius
    c_ref[...] = jnp.broadcast_to(1.0 / jnp.sqrt(jnp.sqrt(frobenius)), c_ref.shape)
    for r in tiles(n):
        m = m0_ref[r] * inverse
        m0_ref[r] = m
        m0b[r] = m.astype(jnp.bfloat16)
    quintic(m0_ref, m0b, w, wb, vb, m1_ref, m1b)


def root_kernel(m0_ref, m1_ref, c_ref, root_out, m0b, m1b, w, wb, vb, m2, m2b):
    n = m0_ref.shape[0]
    for r in tiles(n):
        m0b[r] = m0_ref[r].astype(jnp.bfloat16)
        m1b[r] = m1_ref[r].astype(jnp.bfloat16)
    quintic(m1_ref, m1b, w, wb, vb, m2, m2b)
    c = c_ref[0:1, 0:1] * (1.0 / 64.0)
    for r in tiles(n):
        h = 5.0 * (m0_ref[r] + m1_ref[r]) - dot(m0b[r], m1b[...])
        x = dot(h.astype(jnp.bfloat16), m2b[...]) - 5.0 * h - 25.0 * m2[r]
        x += jnp.where(eye_rows(r, n), 125.0, 0.0)
        root_out[r] = (c * x).astype(jnp.bfloat16)


def cost(flops, moved):
    return pl.CostEstimate(flops=flops, bytes_accessed=moved, transcendentals=0)


def grant(moved):
    return pltpu.CompilerParams(vmem_limit_bytes=max(moved, 1 << 20))


def local(groups, replicas, grad_parts, owner_order, step_count, stat_old, root_old):
    go, gi = halves(groups)
    ro, ri = halves(replicas)
    blocks, rows, width = grad_parts.shape[1:]
    hop = functools.partial(send, groups=groups, replicas=replicas)

    pair = jax.ShapeDtypeStruct((ri, rows, width), jnp.bfloat16)
    picked = pl.pallas_call(
        functools.partial(pick_kernel, replicas),
        out_shape=[pair] * ro,
        in_specs=[SMEM, ANY],
        out_specs=[ANY] * ro,
        scratch_shapes=[pltpu.SemaphoreType.DMA((ro, ri))],
        compiler_params=grant(0),
    )(owner_order, grad_parts[0])

    partial = picked[0].astype(jnp.float32)
    arrived = [hop(picked[k], dg=(0, 0), dr=(k, 0)) for k in range(1, ro)]
    for piece in arrived:
        partial = partial + piece.astype(jnp.float32)

    lots = []
    for a in range(go):
        lot = None
        for d in range(ri):
            piece = partial[d]
            if a or d:
                piece = hop(piece, dg=(a, 0), dr=(0, d))
            lot = piece if lot is None else lot + piece
        lots.append(lot)
    mine = jnp.concatenate(lots, axis=0)
    other = jnp.concatenate([hop(mine, dg=(0, b), dr=(0, 0)) for b in range(1, gi)], axis=0)

    scaled = pl.pallas_call(
        functools.partial(graft_kernel, rows),
        out_shape=jax.ShapeDtypeStruct((rows, width), jnp.bfloat16),
        in_specs=[VMEM] * 3,
        out_specs=VMEM,
        cost_estimate=cost(2 * rows * groups * width * width, 4 * rows * groups * width),
        compiler_params=grant(16 * rows * groups * width + 4 * width * width),
    )(mine, other, root_old[0])

    inner = [scaled] + [hop(scaled, dg=(0, 0), dr=(0, d)) for d in range(1, ri)]
    inner = jnp.stack(inner)
    outer = [inner] + [hop(inner, dg=(0, 0), dr=(k, 0)) for k in range(1, ro)]

    corr = 1.0 / (1.0 - decay_rate ** step_count.astype(jnp.float32))
    square = jax.ShapeDtypeStruct((width, width), jnp.float32)
    f32, bf16 = pltpu.VMEM((width, width), jnp.float32), pltpu.VMEM((width, width), jnp.bfloat16)
    stat_new, m0, m1, c = pl.pallas_call(
        stat_kernel,
        out_shape=[square, square, square, jax.ShapeDtypeStruct((8, 128), jnp.float32)],
        in_specs=[SMEM] + [VMEM] * 3,
        out_specs=[VMEM] * 4,
        scratch_shapes=[bf16, f32, bf16, bf16, bf16],
        cost_estimate=cost(6 * width**3, 12 * width * width),
        compiler_params=grant(48 * width * width),
    )(corr, mine, other, stat_old[0])
    root_new = pl.pallas_call(
        root_kernel,
        out_shape=jax.ShapeDtypeStruct((width, width), jnp.bfloat16),
        in_specs=[VMEM] * 3,
        out_specs=VMEM,
        scratch_shapes=[bf16, bf16, f32, bf16, bf16, f32, bf16],
        cost_estimate=cost(10 * width**3, 8 * width * width),
        compiler_params=grant(48 * width * width),
    )(m0, m1, c)

    update = pl.pallas_call(
        functools.partial(place_kernel, replicas),
        out_shape=jax.ShapeDtypeStruct((blocks, rows, width), jnp.bfloat16),
        in_specs=[SMEM] + [ANY] * ro,
        out_specs=ANY,
        scratch_shapes=[pltpu.SemaphoreType.DMA((ro, ri))],
        compiler_params=grant(0),
    )(owner_order, *outer)
    return (update, stat_new[None], root_new[None])


def solution(mesh):
    placed = (
        P("replica", None, "group", None),
        P(),
        P(),
        P("replica", None, None),
        P("replica", None, None),
    )
    return jax.shard_map(
        functools.partial(local, mesh.shape["group"], mesh.shape["replica"]),
        mesh=mesh,
        in_specs=placed,
        out_specs=(P(None, "group", None), P("replica", None, None), P("replica", None, None)),
        check_vma=False,
    )
```

```python
import functools

import jax
import jax.numpy as jnp
from jax import lax
from jax.experimental import pallas as pl
from jax.experimental.pallas import tpu as pltpu
from jax.sharding import PartitionSpec as P


decay_rate = 0.95
epsilon = 0.001

VMEM = pl.BlockSpec(memory_space=pltpu.VMEM)
SMEM = pl.BlockSpec(memory_space=pltpu.SMEM)
ANY = pl.BlockSpec(memory_space=pl.ANY)
HBM = pl.BlockSpec(memory_space=pltpu.HBM)


def halves(size):
    inner = 2 if size % 2 == 0 else 1
    return size // inner, inner


def is_power(n):
    return n & (n - 1) == 0


def ahead(i, k, n):
    if is_power(n):
        return i ^ k
    return (i + k) % n


def traced_behind(i, k, n):
    return lax.bitwise_xor(i, jnp.int32(k)) if is_power(n) else lax.rem(i + (n - k), n)


def traced_ahead(i, k, n):
    return lax.bitwise_xor(i, jnp.int32(k)) if is_power(n) else lax.rem(i + k, n)


def farthest_first(n):
    return [k for k in range(n - 1, 0, -1)]


def halfway_first(n):
    middle = n // 2
    return [k for k in range(middle, n) if k] + [k for k in range(1, middle)]


def send(x, groups, replicas, dg, dr):
    go, gi = halves(groups)
    ro, ri = halves(replicas)
    pairs = []
    for a in range(go):
        for b in range(gi):
            for c in range(ro):
                for d in range(ri):
                    source = (a * gi + b) * replicas + c * ri + d
                    other_group = ahead(a, dg[0], go) * gi + ahead(b, dg[1], gi)
                    other_replica = ahead(c, dr[0], ro) * ri + ahead(d, dr[1], ri)
                    pairs.append((source, other_group * replicas + other_replica))
    return lax.ppermute(x, ("group", "replica"), pairs)


def pick_kernel(replicas, order_hbm, grads_ref, *rest):
    ro, ri = halves(replicas)
    outs, row_ref = rest[:ro], rest[ro]
    held, order_ref, sem, order_sem = rest[ro + 1 :]
    copy = pltpu.make_async_copy(grads_ref, held, sem)
    copy.start()
    order_copy = pltpu.make_async_copy(order_hbm, order_ref, order_sem)
    order_copy.start()
    me = lax.axis_index("replica")
    outer, inner = lax.div(me, ri), lax.rem(me, ri)
    order_copy.wait()
    positions = lax.broadcasted_iota(jnp.int32, row_ref.shape, 1)
    row = jnp.zeros(row_ref.shape, jnp.int32)
    for slot in range(replicas):
        row = jnp.where(positions == slot, order_ref[slot], row)
    row_ref[...] = row
    copy.wait()
    for k in range(ro):
        for d in range(ri):
            slot = traced_ahead(outer, k, ro) * ri + traced_ahead(inner, d, ri)
            outs[k][d] = held[order_ref[slot]]


def place_kernel(replicas, lots, row_ref, *rest):
    ro, ri = halves(replicas)
    inputs, out_ref, sem = rest[: len(lots)], rest[len(lots)], rest[len(lots) + 1]
    me = lax.axis_index("replica")
    outer, inner = lax.div(me, ri), lax.rem(me, ri)
    row = row_ref[...].astype(jnp.float32)
    positions = lax.broadcasted_iota(jnp.int32, row.shape, 1)
    copies = []
    for ref, offsets in zip(inputs, lots):
        for j, (k, d) in enumerate(offsets):
            slot = traced_behind(outer, k, ro) * ri + traced_behind(inner, d, ri)
            block = jnp.sum(jnp.where(positions == slot, row, 0.0)).astype(jnp.int32)
            copy = pltpu.make_async_copy(ref.at[j], out_ref.at[block], sem.at[len(copies)])
            copy.start()
            copies.append(copy)
    for copy in copies:
        copy.wait()


def graft_kernel(rows, mine_ref, other_ref, root_ref, out_ref):
    mine = mine_ref[...]
    other = other_ref[...]
    root = root_ref[...]
    mine_products = jnp.dot(mine.astype(jnp.bfloat16), root, preferred_element_type=jnp.float32)
    other_products = jnp.dot(other.astype(jnp.bfloat16), root, preferred_element_type=jnp.float32)

    def total(a, b):
        lines = jnp.sum(a * a, axis=0, keepdims=True) + jnp.sum(b * b, axis=0, keepdims=True)
        return jnp.sum(lines, axis=1, keepdims=True)

    graft = jnp.sqrt(total(mine, other) / (total(mine_products, other_products) + 1e-06))
    out_ref[...] = (graft * mine_products[:rows]).astype(jnp.bfloat16)


def dot(a, b):
    return jnp.dot(a, b, preferred_element_type=jnp.float32)


def tiles(n):
    step = 128 if n % 128 == 0 else n
    return [slice(r, r + step) for r in range(0, n, step)]


def square(m_ref, mb_ref, w_ref, wb_ref):
    for r in tiles(m_ref.shape[0]):
        w = 10.0 * m_ref[r] - dot(mb_ref[r], mb_ref[...])
        w_ref[r] = w
        wb_ref[r] = w.astype(jnp.bfloat16)


def quintic(m_ref, mb_ref, w_ref, wb_ref, vb_ref, out_ref, outb_ref):
    n = m_ref.shape[0]
    for r in tiles(n):
        vb_ref[r] = (dot(wb_ref[r], wb_ref[...]) - 50.0 * w_ref[r]).astype(jnp.bfloat16)
    for r in tiles(n):
        m = (625.0 * m_ref[r] + dot(vb_ref[r], mb_ref[...])) * (1.0 / 256.0)
        out_ref[r] = m
        outb_ref[r] = m.astype(jnp.bfloat16)


def eye_rows(r, n):
    rows = lax.broadcasted_iota(jnp.int32, (r.stop - r.start, n), 0) + r.start
    columns = lax.broadcasted_iota(jnp.int32, (r.stop - r.start, n), 1)
    return rows == columns


def stat_kernel(
    corr_ref, mine_ref, other_ref, stat_ref, stat_out, m0, m0b, m1_ref, m1b_ref, c_ref, w, wb, vb
):
    n = stat_ref.shape[0]
    s = jnp.concatenate([mine_ref[...], other_ref[...]], axis=0)
    high = s.astype(jnp.bfloat16)
    low = (s - high.astype(jnp.float32)).astype(jnp.bfloat16)
    left = jnp.concatenate([high, low, high], axis=0)
    right = jnp.concatenate([high, high, low], axis=0)
    corr = corr_ref[0]
    total = jnp.zeros((1, n), jnp.float32)
    for r in tiles(n):
        gram = lax.dot_general(
            left[:, r], right, (((0,), (0,)), ((), ())), preferred_element_type=jnp.float32
        )
        stat = decay_rate * stat_ref[r] + (1.0 - decay_rate) * gram
        stat_out[r] = stat
        shifted = stat * corr + jnp.where(eye_rows(r, n), epsilon, 0.0)
        m0[r] = shifted
        total += jnp.sum(shifted * shifted, axis=0, keepdims=True)
    frobenius = jnp.sqrt(jnp.sum(total, axis=1, keepdims=True))
    inverse = 1.0 / frobenius
    c_ref[...] = jnp.broadcast_to(1.0 / jnp.sqrt(jnp.sqrt(frobenius)), c_ref.shape)
    for r in tiles(n):
        m = m0[r] * inverse
        m0[r] = m
        m0b[r] = m.astype(jnp.bfloat16)
    square(m0, m0b, w, wb)
    quintic(m0, m0b, w, wb, vb, m1_ref, m1b_ref)


def root_kernel(m0, m0b, m1_ref, m1b_ref, c_ref, root_out, w, wb, vb, m2, m2b):
    n = m1_ref.shape[0]
    square(m1_ref, m1b_ref, w, wb)
    quintic(m1_ref, m1b_ref, w, wb, vb, m2, m2b)
    c = c_ref[0:1, 0:1] * (1.0 / 64.0)
    for r in tiles(n):
        h = 5.0 * (m0[r] + m1_ref[r]) - dot(m0b[r], m1b_ref[...])
        x = dot(h.astype(jnp.bfloat16), m2b[...]) - 5.0 * h - 25.0 * m2[r]
        x += jnp.where(eye_rows(r, n), 125.0, 0.0)
        root_out[r] = (c * x).astype(jnp.bfloat16)


def cost(flops, moved):
    return pl.CostEstimate(flops=flops, bytes_accessed=moved, transcendentals=0)


def stay(x):
    return pltpu.with_memory_space_constraint(x, pltpu.HBM)


def grant(moved):
    return pltpu.CompilerParams(vmem_limit_bytes=max(moved, 1 << 20))


def step(groups, replicas, grad_parts, owner_order, step_count, stat_old, root_old):
    go, gi = halves(groups)
    ro, ri = halves(replicas)
    blocks, rows, width = grad_parts.shape[1:]
    hop = functools.partial(send, groups=groups, replicas=replicas)

    pair = jax.ShapeDtypeStruct((ri, rows, width), jnp.bfloat16)
    lanes = 128 * pl.cdiv(replicas, 128)
    *picked, row = pl.pallas_call(
        functools.partial(pick_kernel, replicas),
        out_shape=[pair] * ro + [jax.ShapeDtypeStruct((1, lanes), jnp.int32)],
        in_specs=[HBM, HBM],
        out_specs=[VMEM] * (ro + 1),
        scratch_shapes=[
            pltpu.VMEM((blocks, rows, width), jnp.bfloat16),
            pltpu.SMEM((replicas,), jnp.int32),
            pltpu.SemaphoreType.DMA,
            pltpu.SemaphoreType.DMA,
        ],
        compiler_params=grant(8 * blocks * rows * width),
    )(stay(owner_order), stay(grad_parts[0]))

    partial = picked[0].astype(jnp.float32)
    for k in halfway_first(ro):
        partial = partial + hop(picked[k], dg=(0, 0), dr=(k, 0)).astype(jnp.float32)

    offsets = [(a, d) for a in range(go) for d in range(ri)]
    pieces = {(0, 0): partial[0]}
    for a, d in offsets[1:]:
        pieces[a, d] = hop(partial[d], dg=(a, 0), dr=(0, d))
    lots = [sum((pieces[a, d] for d in range(1, ri)), pieces[a, 0]) for a in range(go)]
    mine = jnp.concatenate(lots, axis=0)
    other = jnp.concatenate([hop(mine, dg=(0, b), dr=(0, 0)) for b in range(1, gi)], axis=0)

    scaled = pl.pallas_call(
        functools.partial(graft_kernel, rows),
        out_shape=jax.ShapeDtypeStruct((rows, width), jnp.bfloat16),
        in_specs=[VMEM] * 3,
        out_specs=VMEM,
        cost_estimate=cost(2 * rows * groups * width * width, 4 * rows * groups * width),
        compiler_params=grant(16 * rows * groups * width + 4 * width * width),
    )(mine, other, root_old[0])

    ks, ds = farthest_first(ro), list(range(1, ri))
    came = []
    for k in ks:
        came.append(hop(scaled, dg=(0, 0), dr=(k, 0)))
    lots = [(scaled[None], [(0, 0)])]
    for d in ds:
        lots.append((hop(scaled, dg=(0, 0), dr=(0, d))[None], [(0, d)]))
    came = jnp.stack(came)
    lots.append((came, [(k, 0) for k in ks]))
    for d in ds:
        lots.append((hop(came, dg=(0, 0), dr=(0, d)), [(k, d) for k in ks]))

    corr = 1.0 / (1.0 - decay_rate ** step_count.astype(jnp.float32))
    full, half = jax.ShapeDtypeStruct((width, width), jnp.float32), jax.ShapeDtypeStruct((width, width), jnp.bfloat16)
    f32, bf16 = pltpu.VMEM(full.shape, full.dtype), pltpu.VMEM(half.shape, half.dtype)
    stat_new, *held = pl.pallas_call(
        stat_kernel,
        out_shape=[full, full, half, full, half, jax.ShapeDtypeStruct((8, 128), jnp.float32)],
        in_specs=[SMEM] + [VMEM] * 3,
        out_specs=[VMEM] * 6,
        scratch_shapes=[f32, bf16, bf16],
        cost_estimate=cost(10 * width**3, 12 * width * width),
        compiler_params=grant(64 * width * width),
    )(corr, mine, other, stat_old[0])
    root_new = pl.pallas_call(
        root_kernel,
        out_shape=half,
        in_specs=[VMEM] * 5,
        out_specs=VMEM,
        scratch_shapes=[f32, bf16, bf16, f32, bf16],
        cost_estimate=cost(6 * width**3, 8 * width * width),
        compiler_params=grant(48 * width * width),
    )(*held)

    update = pl.pallas_call(
        functools.partial(place_kernel, replicas, [offsets for _, offsets in lots]),
        out_shape=jax.ShapeDtypeStruct((blocks, rows, width), jnp.bfloat16),
        in_specs=[VMEM] + [ANY] * len(lots),
        out_specs=ANY,
        scratch_shapes=[pltpu.SemaphoreType.DMA((replicas,))],
        compiler_params=grant(0),
    )(row, *[lot for lot, _ in lots])
    return (update, stat_new[None], root_new[None])


def solution(mesh):
    placed = (
        P("replica", None, "group", None),
        P(),
        P(),
        P("replica", None, None),
        P("replica", None, None),
    )
    return jax.shard_map(
        functools.partial(step, mesh.shape["group"], mesh.shape["replica"]),
        mesh=mesh,
        in_specs=placed,
        out_specs=(P(None, "group", None), P("replica", None, None), P("replica", None, None)),
        check_vma=False,
    )
```

```python
import functools

import jax
import jax.numpy as jnp
from jax import lax
from jax.experimental import pallas as pl
from jax.experimental.pallas import tpu as pltpu
from jax.sharding import PartitionSpec as P


decay_rate = 0.95
epsilon = 0.001

VMEM = pl.BlockSpec(memory_space=pltpu.VMEM)
SMEM = pl.BlockSpec(memory_space=pltpu.SMEM)
ANY = pl.BlockSpec(memory_space=pl.ANY)
HBM = pl.BlockSpec(memory_space=pltpu.HBM)


def halves(size):
    inner = 2 if size % 2 == 0 else 1
    return size // inner, inner


def is_power(n):
    return n & (n - 1) == 0


def ahead(i, k, n):
    if is_power(n):
        return i ^ k
    return (i + k) % n


def traced_behind(i, k, n):
    return lax.bitwise_xor(i, jnp.int32(k)) if is_power(n) else lax.rem(i + (n - k), n)


def traced_ahead(i, k, n):
    return lax.bitwise_xor(i, jnp.int32(k)) if is_power(n) else lax.rem(i + k, n)


def farthest_first(n):
    return [k for k in range(n - 1, 0, -1)]


def halfway_first(n):
    middle = n // 2
    return [k for k in range(middle, n) if k] + [k for k in range(1, middle)]


def send(x, groups, replicas, dg, dr):
    go, gi = halves(groups)
    ro, ri = halves(replicas)
    pairs = []
    for a in range(go):
        for b in range(gi):
            for c in range(ro):
                for d in range(ri):
                    source = (a * gi + b) * replicas + c * ri + d
                    other_group = ahead(a, dg[0], go) * gi + ahead(b, dg[1], gi)
                    other_replica = ahead(c, dr[0], ro) * ri + ahead(d, dr[1], ri)
                    pairs.append((source, other_group * replicas + other_replica))
    return lax.ppermute(x, ("group", "replica"), pairs)


def pick_kernel(replicas, order_hbm, grads_ref, *rest):
    ro, ri = halves(replicas)
    outs, row_ref = rest[:ro], rest[ro]
    held, order_ref, sem, order_sem = rest[ro + 1 :]
    copy = pltpu.make_async_copy(grads_ref, held, sem)
    copy.start()
    order_copy = pltpu.make_async_copy(order_hbm, order_ref, order_sem)
    order_copy.start()
    me = lax.axis_index("replica")
    outer, inner = lax.div(me, ri), lax.rem(me, ri)
    order_copy.wait()
    positions = lax.broadcasted_iota(jnp.int32, row_ref.shape, 1)
    row = jnp.zeros(row_ref.shape, jnp.int32)
    for slot in range(replicas):
        row = jnp.where(positions == slot, order_ref[slot], row)
    row_ref[...] = row
    copy.wait()
    for k in range(ro):
        for d in range(ri):
            slot = traced_ahead(outer, k, ro) * ri + traced_ahead(inner, d, ri)
            outs[k][d] = held[order_ref[slot]]


def place_kernel(replicas, lots, row_ref, *rest):
    ro, ri = halves(replicas)
    inputs, out_ref, sem = rest[: len(lots)], rest[len(lots)], rest[len(lots) + 1]
    me = lax.axis_index("replica")
    outer, inner = lax.div(me, ri), lax.rem(me, ri)
    row = row_ref[...].astype(jnp.float32)
    positions = lax.broadcasted_iota(jnp.int32, row.shape, 1)
    copies = []
    for ref, offsets in zip(inputs, lots):
        for j, (k, d) in enumerate(offsets):
            slot = traced_behind(outer, k, ro) * ri + traced_behind(inner, d, ri)
            block = jnp.sum(jnp.where(positions == slot, row, 0.0)).astype(jnp.int32)
            copy = pltpu.make_async_copy(ref.at[j], out_ref.at[block], sem.at[len(copies)])
            copy.start()
            copies.append(copy)
    for copy in copies:
        copy.wait()


def product_kernel(rows, mine_ref, root_ref, product_ref, norm_ref):
    mine = mine_ref[...]
    products = dot(mine.astype(jnp.bfloat16), root_ref[...])
    product_ref[...] = products[:rows]
    for row, x in enumerate((mine, products)):
        total = jnp.sum(jnp.sum(x * x, axis=0, keepdims=True), axis=1, keepdims=True)
        norm_ref[row : row + 1] = jnp.broadcast_to(total, (1, norm_ref.shape[1]))


def graft_kernel(other_ref, root_ref, product_ref, norm_ref, out_ref):
    other = other_ref[...]
    others = dot(other.astype(jnp.bfloat16), root_ref[...])

    def total(x):
        return jnp.sum(jnp.sum(x * x, axis=0, keepdims=True), axis=1, keepdims=True)

    grad_norm = norm_ref[0:1, 0:1] + total(other)
    update_norm = norm_ref[1:2, 0:1] + total(others)
    graft = jnp.sqrt(grad_norm / (update_norm + 1e-06))
    out_ref[...] = (graft * product_ref[...]).astype(jnp.bfloat16)


def dot(a, b):
    return jnp.dot(a, b, preferred_element_type=jnp.float32)


def tiles(n):
    step = 128 if n % 128 == 0 else n
    return [slice(r, r + step) for r in range(0, n, step)]


def square(m_ref, mb_ref, w_ref, wb_ref):
    for r in tiles(m_ref.shape[0]):
        w = 10.0 * m_ref[r] - dot(mb_ref[r], mb_ref[...])
        w_ref[r] = w
        wb_ref[r] = w.astype(jnp.bfloat16)


def quintic(m_ref, mb_ref, w_ref, wb_ref, vb_ref, out_ref, outb_ref):
    n = m_ref.shape[0]
    for r in tiles(n):
        vb_ref[r] = (dot(wb_ref[r], wb_ref[...]) - 50.0 * w_ref[r]).astype(jnp.bfloat16)
    for r in tiles(n):
        m = (625.0 * m_ref[r] + dot(vb_ref[r], mb_ref[...])) * (1.0 / 256.0)
        out_ref[r] = m
        outb_ref[r] = m.astype(jnp.bfloat16)


def eye_rows(r, n):
    rows = lax.broadcasted_iota(jnp.int32, (r.stop - r.start, n), 0) + r.start
    columns = lax.broadcasted_iota(jnp.int32, (r.stop - r.start, n), 1)
    return rows == columns


def stat_kernel(
    corr_ref, mine_ref, other_ref, stat_ref, stat_out, m0, m0b, m1_ref, m1b_ref, c_ref, w, wb, vb
):
    n = stat_ref.shape[0]
    s = jnp.concatenate([mine_ref[...], other_ref[...]], axis=0)
    high = s.astype(jnp.bfloat16)
    low = (s - high.astype(jnp.float32)).astype(jnp.bfloat16)
    left = jnp.concatenate([high, low, high], axis=0)
    right = jnp.concatenate([high, high, low], axis=0)
    corr = corr_ref[0]
    total = jnp.zeros((1, n), jnp.float32)
    for r in tiles(n):
        gram = lax.dot_general(
            left[:, r], right, (((0,), (0,)), ((), ())), preferred_element_type=jnp.float32
        )
        stat = decay_rate * stat_ref[r] + (1.0 - decay_rate) * gram
        stat_out[r] = stat
        shifted = stat * corr + jnp.where(eye_rows(r, n), epsilon, 0.0)
        m0[r] = shifted
        total += jnp.sum(shifted * shifted, axis=0, keepdims=True)
    frobenius = jnp.sqrt(jnp.sum(total, axis=1, keepdims=True))
    inverse = 1.0 / frobenius
    c_ref[...] = jnp.broadcast_to(1.0 / jnp.sqrt(jnp.sqrt(frobenius)), c_ref.shape)
    for r in tiles(n):
        m = m0[r] * inverse
        m0[r] = m
        m0b[r] = m.astype(jnp.bfloat16)
    square(m0, m0b, w, wb)
    quintic(m0, m0b, w, wb, vb, m1_ref, m1b_ref)


def root_kernel(m0, m0b, m1_ref, m1b_ref, c_ref, root_out, w, wb, vb, m2, m2b):
    n = m1_ref.shape[0]
    square(m1_ref, m1b_ref, w, wb)
    quintic(m1_ref, m1b_ref, w, wb, vb, m2, m2b)
    c = c_ref[0:1, 0:1] * (1.0 / 64.0)
    for r in tiles(n):
        h = 5.0 * (m0[r] + m1_ref[r]) - dot(m0b[r], m1b_ref[...])
        x = dot(h.astype(jnp.bfloat16), m2b[...]) - 5.0 * h - 25.0 * m2[r]
        x += jnp.where(eye_rows(r, n), 125.0, 0.0)
        root_out[r] = (c * x).astype(jnp.bfloat16)


def cost(flops, moved):
    return pl.CostEstimate(flops=flops, bytes_accessed=moved, transcendentals=0)


def stay(x):
    return pltpu.with_memory_space_constraint(x, pltpu.HBM)


def grant(moved):
    return pltpu.CompilerParams(vmem_limit_bytes=max(moved, 1 << 20))


def step(groups, replicas, grad_parts, owner_order, step_count, stat_old, root_old):
    go, gi = halves(groups)
    ro, ri = halves(replicas)
    blocks, rows, width = grad_parts.shape[1:]
    hop = functools.partial(send, groups=groups, replicas=replicas)

    pair = jax.ShapeDtypeStruct((ri, rows, width), jnp.bfloat16)
    lanes = 128 * pl.cdiv(replicas, 128)
    *picked, row = pl.pallas_call(
        functools.partial(pick_kernel, replicas),
        out_shape=[pair] * ro + [jax.ShapeDtypeStruct((1, lanes), jnp.int32)],
        in_specs=[HBM, HBM],
        out_specs=[VMEM] * (ro + 1),
        scratch_shapes=[
            pltpu.VMEM((blocks, rows, width), jnp.bfloat16),
            pltpu.SMEM((replicas,), jnp.int32),
            pltpu.SemaphoreType.DMA,
            pltpu.SemaphoreType.DMA,
        ],
        compiler_params=grant(8 * blocks * rows * width),
    )(stay(owner_order), stay(grad_parts[0]))

    partial = picked[0].astype(jnp.float32)
    for k in halfway_first(ro):
        partial = partial + hop(picked[k], dg=(0, 0), dr=(k, 0)).astype(jnp.float32)

    offsets = [(a, d) for a in range(go) for d in range(ri)]
    pieces = {(0, 0): partial[0]}
    for a, d in offsets[1:]:
        pieces[a, d] = hop(partial[d], dg=(a, 0), dr=(0, d))
    lots = [sum((pieces[a, d] for d in range(1, ri)), pieces[a, 0]) for a in range(go)]
    mine = jnp.concatenate(lots, axis=0)
    others = []
    for b in range(1, gi):
        others.append(hop(mine, dg=(0, b), dr=(0, 0)))
    other = jnp.concatenate(others, axis=0)

    products, norms = pl.pallas_call(
        functools.partial(product_kernel, rows),
        out_shape=[jax.ShapeDtypeStruct((rows, width), jnp.float32), jax.ShapeDtypeStruct((2, 128), jnp.float32)],
        in_specs=[VMEM] * 2,
        out_specs=[VMEM] * 2,
        cost_estimate=cost(2 * rows * go * width * width, 4 * rows * go * width),
        compiler_params=grant(16 * rows * groups * width + 4 * width * width),
    )(mine, root_old[0])
    scaled = pl.pallas_call(
        graft_kernel,
        out_shape=jax.ShapeDtypeStruct((rows, width), jnp.bfloat16),
        in_specs=[VMEM] * 4,
        out_specs=VMEM,
        cost_estimate=cost(2 * rows * groups * width * width, 4 * rows * groups * width),
        compiler_params=grant(16 * rows * groups * width + 4 * width * width),
    )(other, root_old[0], products, norms)

    ks, ds = farthest_first(ro), list(range(1, ri))
    came = []
    for k in ks:
        came.append(hop(scaled, dg=(0, 0), dr=(k, 0)))
    lots = [(scaled[None], [(0, 0)])]
    for d in ds:
        lots.append((hop(scaled, dg=(0, 0), dr=(0, d))[None], [(0, d)]))
    came = jnp.stack(came)
    lots.append((came, [(k, 0) for k in ks]))
    for d in ds:
        lots.append((hop(came, dg=(0, 0), dr=(0, d)), [(k, d) for k in ks]))

    corr = 1.0 / (1.0 - decay_rate ** step_count.astype(jnp.float32))
    full, half = jax.ShapeDtypeStruct((width, width), jnp.float32), jax.ShapeDtypeStruct((width, width), jnp.bfloat16)
    f32, bf16 = pltpu.VMEM(full.shape, full.dtype), pltpu.VMEM(half.shape, half.dtype)
    stat_new, *held = pl.pallas_call(
        stat_kernel,
        out_shape=[full, full, half, full, half, jax.ShapeDtypeStruct((8, 128), jnp.float32)],
        in_specs=[SMEM] + [VMEM] * 3,
        out_specs=[VMEM] * 6,
        scratch_shapes=[f32, bf16, bf16],
        cost_estimate=cost(10 * width**3, 12 * width * width),
        compiler_params=grant(64 * width * width),
    )(corr, mine, other, stat_old[0])
    root_new = pl.pallas_call(
        root_kernel,
        out_shape=half,
        in_specs=[VMEM] * 5,
        out_specs=VMEM,
        scratch_shapes=[f32, bf16, bf16, f32, bf16],
        cost_estimate=cost(6 * width**3, 8 * width * width),
        compiler_params=grant(48 * width * width),
    )(*held)

    update = pl.pallas_call(
        functools.partial(place_kernel, replicas, [offsets for _, offsets in lots]),
        out_shape=jax.ShapeDtypeStruct((blocks, rows, width), jnp.bfloat16),
        in_specs=[VMEM] + [ANY] * len(lots),
        out_specs=ANY,
        scratch_shapes=[pltpu.SemaphoreType.DMA((replicas,))],
        compiler_params=grant(0),
    )(row, *[lot for lot, _ in lots])
    return (update, stat_new[None], root_new[None])


def solution(mesh):
    placed = (
        P("replica", None, "group", None),
        P(),
        P(),
        P("replica", None, None),
        P("replica", None, None),
    )
    return jax.shard_map(
        functools.partial(step, mesh.shape["group"], mesh.shape["replica"]),
        mesh=mesh,
        in_specs=placed,
        out_specs=(P(None, "group", None), P("replica", None, None), P("replica", None, None)),
        check_vma=False,
    )
```

```python
import functools

import jax
import jax.numpy as jnp
from jax import lax
from jax.experimental import pallas as pl
from jax.experimental.pallas import tpu as pltpu
from jax.sharding import PartitionSpec as P


decay_rate = 0.95
epsilon = 0.001

VMEM = pl.BlockSpec(memory_space=pltpu.VMEM)
SMEM = pl.BlockSpec(memory_space=pltpu.SMEM)
ANY = pl.BlockSpec(memory_space=pl.ANY)
HBM = pl.BlockSpec(memory_space=pltpu.HBM)


def halves(size):
    inner = 2 if size % 2 == 0 else 1
    return size // inner, inner


def is_power(n):
    return n & (n - 1) == 0


def ahead(i, k, n):
    if is_power(n):
        return i ^ k
    return (i + k) % n


def traced_behind(i, k, n):
    return lax.bitwise_xor(i, jnp.int32(k)) if is_power(n) else lax.rem(i + (n - k), n)


def traced_ahead(i, k, n):
    return lax.bitwise_xor(i, jnp.int32(k)) if is_power(n) else lax.rem(i + k, n)


def farthest_first(n):
    return [k for k in range(n - 1, 0, -1)]


def send(x, groups, replicas, dg, dr):
    go, gi = halves(groups)
    ro, ri = halves(replicas)
    pairs = []
    for a in range(go):
        for b in range(gi):
            for c in range(ro):
                for d in range(ri):
                    source = (a * gi + b) * replicas + c * ri + d
                    other_group = ahead(a, dg[0], go) * gi + ahead(b, dg[1], gi)
                    other_replica = ahead(c, dr[0], ro) * ri + ahead(d, dr[1], ri)
                    pairs.append((source, other_group * replicas + other_replica))
    return lax.ppermute(x, ("group", "replica"), pairs)


def pick_kernel(replicas, order_hbm, grads_ref, *rest):
    ro, ri = halves(replicas)
    outs, row_ref = rest[:ro], rest[ro]
    held, order_ref, sem, order_sem = rest[ro + 1 :]
    copy = pltpu.make_async_copy(grads_ref, held, sem)
    copy.start()
    order_copy = pltpu.make_async_copy(order_hbm, order_ref, order_sem)
    order_copy.start()
    me = lax.axis_index("replica")
    outer, inner = lax.div(me, ri), lax.rem(me, ri)
    order_copy.wait()
    positions = lax.broadcasted_iota(jnp.int32, row_ref.shape, 1)
    row = jnp.zeros(row_ref.shape, jnp.int32)
    for slot in range(replicas):
        row = jnp.where(positions == slot, order_ref[slot], row)
    row_ref[...] = row
    copy.wait()
    for k in range(ro):
        for d in range(ri):
            slot = traced_ahead(outer, k, ro) * ri + traced_ahead(inner, d, ri)
            outs[k][d] = held[order_ref[slot]]


def place_kernel(replicas, lots, row_ref, *rest):
    ro, ri = halves(replicas)
    inputs, out_ref, sem = rest[: len(lots)], rest[len(lots)], rest[len(lots) + 1]
    me = lax.axis_index("replica")
    outer, inner = lax.div(me, ri), lax.rem(me, ri)
    row = row_ref[...].astype(jnp.float32)
    positions = lax.broadcasted_iota(jnp.int32, row.shape, 1)
    copies = []
    for ref, offsets in zip(inputs, lots):
        for j, (k, d) in enumerate(offsets):
            slot = traced_behind(outer, k, ro) * ri + traced_behind(inner, d, ri)
            block = jnp.sum(jnp.where(positions == slot, row, 0.0)).astype(jnp.int32)
            copy = pltpu.make_async_copy(ref.at[j], out_ref.at[block], sem.at[len(copies)])
            copy.start()
            copies.append(copy)
    for copy in copies:
        copy.wait()


def graft_kernel(rows, mine_ref, other_ref, root_ref, out_ref):
    mine = mine_ref[...]
    other = other_ref[...]
    root = root_ref[...]
    mine_products = jnp.dot(mine.astype(jnp.bfloat16), root, preferred_element_type=jnp.float32)
    other_products = jnp.dot(other.astype(jnp.bfloat16), root, preferred_element_type=jnp.float32)

    def total(a, b):
        lines = jnp.sum(a * a, axis=0, keepdims=True) + jnp.sum(b * b, axis=0, keepdims=True)
        return jnp.sum(lines, axis=1, keepdims=True)

    graft = jnp.sqrt(total(mine, other) / (total(mine_products, other_products) + 1e-06))
    out_ref[...] = (graft * mine_products[:rows]).astype(jnp.bfloat16)


def dot(a, b):
    return jnp.dot(a, b, preferred_element_type=jnp.float32)


def tiles(n):
    step = 128 if n % 128 == 0 else n
    return [slice(r, r + step) for r in range(0, n, step)]


def square(m_ref, mb_ref, w_ref, wb_ref):
    for r in tiles(m_ref.shape[0]):
        w = 10.0 * m_ref[r] - dot(mb_ref[r], mb_ref[...])
        w_ref[r] = w
        wb_ref[r] = w.astype(jnp.bfloat16)


def quintic(m_ref, mb_ref, w_ref, wb_ref, vb_ref, out_ref, outb_ref):
    n = m_ref.shape[0]
    for r in tiles(n):
        vb_ref[r] = (dot(wb_ref[r], wb_ref[...]) - 50.0 * w_ref[r]).astype(jnp.bfloat16)
    for r in tiles(n):
        m = (625.0 * m_ref[r] + dot(vb_ref[r], mb_ref[...])) * (1.0 / 256.0)
        out_ref[r] = m
        outb_ref[r] = m.astype(jnp.bfloat16)


def eye_rows(r, n):
    rows = lax.broadcasted_iota(jnp.int32, (r.stop - r.start, n), 0) + r.start
    columns = lax.broadcasted_iota(jnp.int32, (r.stop - r.start, n), 1)
    return rows == columns


def stat_kernel(
    corr_ref, mine_ref, other_ref, stat_ref, stat_out, m0, m0b, m1_ref, m1b_ref, c_ref, w, wb, vb
):
    n = stat_ref.shape[0]
    s = jnp.concatenate([mine_ref[...], other_ref[...]], axis=0)
    high = s.astype(jnp.bfloat16)
    low = (s - high.astype(jnp.float32)).astype(jnp.bfloat16)
    left = jnp.concatenate([high, low, high], axis=0)
    right = jnp.concatenate([high, high, low], axis=0)
    corr = corr_ref[0]
    total = jnp.zeros((1, n), jnp.float32)
    for r in tiles(n):
        gram = lax.dot_general(
            left[:, r], right, (((0,), (0,)), ((), ())), preferred_element_type=jnp.float32
        )
        stat = decay_rate * stat_ref[r] + (1.0 - decay_rate) * gram
        stat_out[r] = stat
        shifted = stat * corr + jnp.where(eye_rows(r, n), epsilon, 0.0)
        m0[r] = shifted
        total += jnp.sum(shifted * shifted, axis=0, keepdims=True)
    frobenius = jnp.sqrt(jnp.sum(total, axis=1, keepdims=True))
    inverse = 1.0 / frobenius
    c_ref[...] = jnp.broadcast_to(1.0 / jnp.sqrt(jnp.sqrt(frobenius)), c_ref.shape)
    for r in tiles(n):
        m = m0[r] * inverse
        m0[r] = m
        m0b[r] = m.astype(jnp.bfloat16)
    square(m0, m0b, w, wb)
    quintic(m0, m0b, w, wb, vb, m1_ref, m1b_ref)


def root_kernel(m0, m0b, m1_ref, m1b_ref, c_ref, root_out, w, wb, vb, m2, m2b):
    n = m1_ref.shape[0]
    square(m1_ref, m1b_ref, w, wb)
    quintic(m1_ref, m1b_ref, w, wb, vb, m2, m2b)
    c = c_ref[0:1, 0:1] * (1.0 / 64.0)
    for r in tiles(n):
        h = 5.0 * (m0[r] + m1_ref[r]) - dot(m0b[r], m1b_ref[...])
        x = dot(h.astype(jnp.bfloat16), m2b[...]) - 5.0 * h - 25.0 * m2[r]
        x += jnp.where(eye_rows(r, n), 125.0, 0.0)
        root_out[r] = (c * x).astype(jnp.bfloat16)


def cost(flops, moved):
    return pl.CostEstimate(flops=flops, bytes_accessed=moved, transcendentals=0)


def stay(x):
    return pltpu.with_memory_space_constraint(x, pltpu.HBM)


def grant(moved):
    return pltpu.CompilerParams(vmem_limit_bytes=max(moved, 1 << 20))


def step(groups, replicas, grad_parts, owner_order, step_count, stat_old, root_old):
    go, gi = halves(groups)
    ro, ri = halves(replicas)
    blocks, rows, width = grad_parts.shape[1:]
    hop = functools.partial(send, groups=groups, replicas=replicas)

    pair = jax.ShapeDtypeStruct((ri, rows, width), jnp.bfloat16)
    lanes = 128 * pl.cdiv(replicas, 128)
    *picked, row = pl.pallas_call(
        functools.partial(pick_kernel, replicas),
        out_shape=[pair] * ro + [jax.ShapeDtypeStruct((1, lanes), jnp.int32)],
        in_specs=[HBM, HBM],
        out_specs=[VMEM] * (ro + 1),
        scratch_shapes=[
            pltpu.VMEM((blocks, rows, width), jnp.bfloat16),
            pltpu.SMEM((replicas,), jnp.int32),
            pltpu.SemaphoreType.DMA,
            pltpu.SemaphoreType.DMA,
        ],
        compiler_params=grant(8 * blocks * rows * width),
    )(stay(owner_order), stay(grad_parts[0]))

    partial = picked[0].astype(jnp.float32)
    for k in farthest_first(ro):
        partial = partial + hop(picked[k], dg=(0, 0), dr=(k, 0)).astype(jnp.float32)

    offsets = [(a, d) for a in range(go) for d in range(ri)]
    pieces = {(0, 0): partial[0]}
    for a, d in offsets[1:]:
        pieces[a, d] = hop(partial[d], dg=(a, 0), dr=(0, d))
    lots = [sum((pieces[a, d] for d in range(1, ri)), pieces[a, 0]) for a in range(go)]
    mine = jnp.concatenate(lots, axis=0)
    other = jnp.concatenate([hop(mine, dg=(0, b), dr=(0, 0)) for b in range(1, gi)], axis=0)

    scaled = pl.pallas_call(
        functools.partial(graft_kernel, rows),
        out_shape=jax.ShapeDtypeStruct((rows, width), jnp.bfloat16),
        in_specs=[VMEM] * 3,
        out_specs=VMEM,
        cost_estimate=cost(2 * rows * groups * width * width, 4 * rows * groups * width),
        compiler_params=grant(16 * rows * groups * width + 4 * width * width),
    )(mine, other, root_old[0])

    ks, ds = farthest_first(ro), list(range(1, ri))
    came = []
    for k in ks:
        came.append(hop(scaled, dg=(0, 0), dr=(k, 0)))
    lots = [(scaled[None], [(0, 0)])]
    for d in ds:
        lots.append((hop(scaled, dg=(0, 0), dr=(0, d))[None], [(0, d)]))
    came = jnp.stack(came)
    lots.append((came, [(k, 0) for k in ks]))
    for d in ds:
        lots.append((hop(came, dg=(0, 0), dr=(0, d)), [(k, d) for k in ks]))

    corr = 1.0 / (1.0 - decay_rate ** step_count.astype(jnp.float32))
    full, half = jax.ShapeDtypeStruct((width, width), jnp.float32), jax.ShapeDtypeStruct((width, width), jnp.bfloat16)
    f32, bf16 = pltpu.VMEM(full.shape, full.dtype), pltpu.VMEM(half.shape, half.dtype)
    stat_new, *held = pl.pallas_call(
        stat_kernel,
        out_shape=[full, full, half, full, half, jax.ShapeDtypeStruct((8, 128), jnp.float32)],
        in_specs=[SMEM] + [VMEM] * 3,
        out_specs=[VMEM] * 6,
        scratch_shapes=[f32, bf16, bf16],
        cost_estimate=cost(10 * width**3, 12 * width * width),
        compiler_params=grant(64 * width * width),
    )(corr, mine, other, stat_old[0])
    root_new = pl.pallas_call(
        root_kernel,
        out_shape=half,
        in_specs=[VMEM] * 5,
        out_specs=VMEM,
        scratch_shapes=[f32, bf16, bf16, f32, bf16],
        cost_estimate=cost(6 * width**3, 8 * width * width),
        compiler_params=grant(48 * width * width),
    )(*held)

    update = pl.pallas_call(
        functools.partial(place_kernel, replicas, [offsets for _, offsets in lots]),
        out_shape=jax.ShapeDtypeStruct((blocks, rows, width), jnp.bfloat16),
        in_specs=[VMEM] + [ANY] * len(lots),
        out_specs=ANY,
        scratch_shapes=[pltpu.SemaphoreType.DMA((replicas,))],
        compiler_params=grant(0),
    )(row, *[lot for lot, _ in lots])
    return (update, stat_new[None], root_new[None])


def solution(mesh):
    placed = (
        P("replica", None, "group", None),
        P(),
        P(),
        P("replica", None, None),
        P("replica", None, None),
    )
    return jax.shard_map(
        functools.partial(step, mesh.shape["group"], mesh.shape["replica"]),
        mesh=mesh,
        in_specs=placed,
        out_specs=(P(None, "group", None), P("replica", None, None), P("replica", None, None)),
        check_vma=False,
    )
```
